32 devices in a mesh: section: 4 (over x, core), fsdp: 8 (over z, y).
Axes of the slice: x: 2, y: 2, z: 4, core: 2. Of those that a mesh axis runs over, the one named last changes fastest.
Arguments:
- section_input: bfloat16 [4, 256, 12288], P('section', None, 'fsdp'), may hold values from -6 to 6
- stash_held: bfloat16 [4, 256, 12288], P('section', None, 'fsdp'), may hold values from -17 to 17
- upstream: bfloat16 [4, 256, 12288], P('section', None, 'fsdp'), may hold values from -6 to 6
- norm_gain: float32 [4, 12288], P('section', 'fsdp'), may hold values from 0.25 to 1.75
- out_weight: bfloat16 [4, 6144, 12288], P('section', None, 'fsdp'), may hold values from -0.078125 to 0.078125
Outputs:
- section_output: bfloat16 [4, 256, 12288], P('section', None, 'fsdp')
- stash_moved: bfloat16 [4, 256, 12288], P('section', None, 'fsdp')
- input_grad: bfloat16 [4, 256, 12288], P('section', None, 'fsdp')
The draws below stay inside these ranges and needn't reach their ends.
All inputs are finite; a program needn't handle non-finite values.
Results may differ from the reference program's by a relative error of at most 0.012.
The reference program's roundings to bfloat16 on the way (of `fetched`, `normed`, `weights`, `context`, `dcontext` and `dscore`) count: a program that leaves them out, or rounds other values in their place, can miss the bound.
Values may be sent and summed in bfloat16 or wider, within the bound.
No kernel may reach another device: no remote copies, remote signals or barrier semaphores. Data moves between devices by JAX's collectives and lax.ppermute only.
A program may use at most 64 MiB of HBM per device.

```python
import math
import jax
import jax.numpy as jnp
from jax import lax

D = 12288
HD = 128
SEQ = 256
SECTIONS = 4


def draw_stash_held(key, part):
    key_base = jax.random.fold_in(key, 11)
    key_rows = jax.random.fold_in(key, 12)
    key_blocks = jax.random.fold_in(key, 13)
    blocks = D // HD
    levels = jnp.exp(jax.random.uniform(key_blocks, (SECTIONS, 1, blocks, 1), jnp.float32, -3.0, 3.0))
    row_scale = jnp.exp(jax.random.uniform(key_rows, (SECTIONS, SEQ, 1, 1), jnp.float32, math.log(0.02), math.log(0.2)))
    base = jax.random.normal(key_base, (SECTIONS, SEQ, blocks, HD), jnp.float32)
    base = jnp.clip(base, -4.0, 4.0)
    values = base * levels * row_scale
    return values.reshape(SECTIONS, SEQ, D).astype(jnp.bfloat16)


def block_scale(own_key, extent, shards, low, top_value):
    factor_of, own = 1.0, jax.random.fold_in(own_key, 6)
    for axis_at, shards_of in shards:
        steps = jnp.exp(jax.random.uniform(jax.random.fold_in(own, axis_at), (shards_of,), jnp.float32, low / len(shards), top_value / len(shards)))
        factor_of = factor_of * jnp.repeat(steps, extent[axis_at] // shards_of).reshape([-1 if axis == axis_at else 1 for axis in range(len(extent))])
    return factor_of


def normal_values(own_key, extent, scale, limit, cuts=(), kind=jnp.bfloat16):
    values = jax.random.normal(own_key, extent, jnp.float32) * scale
    if len(cuts) > 0:
        values = block_scale(own_key, extent, cuts, -0.22, 0.18) * values
    return jnp.clip(values, min=-limit, max=limit).astype(kind)


def setup_inputs(seed: int = 0) -> dict:
    splits = jax.random.split(jax.random.key(seed), 6)
    return {
        "section_input": normal_values(splits[0], (SECTIONS, SEQ, D), 1.0, 6.0, ((0, 4), (2, 8))),
        "stash_held": draw_stash_held(jax.random.fold_in(splits[5], 71), 0),
        "upstream": normal_values(splits[2], (SECTIONS, SEQ, D), 1.0, 6.0, ((0, 4), (2, 8))),
        "norm_gain": jnp.clip(1.0 + 0.15 * jax.random.normal(splits[3], (SECTIONS, D), jnp.float32), 0.25, 1.75),
        "out_weight": normal_values(splits[4], (SECTIONS, D // 2, D), (D // 2) ** -0.5, 0.078125, ((0, 4), (2, 8))),
    }


EPSILON = 1e-05

def attend(normed):
    paired = normed.reshape(SEQ, D // (2 * HD), 2, HD)
    queries = paired[:, :, 0].astype(jnp.float32)
    keyvals = paired[:, :, 1].astype(jnp.float32)
    shrink = HD ** (-0.5)
    scores = jnp.einsum('qhd,khd->hqk', queries, keyvals) * shrink
    allowed = jnp.arange(SEQ)[:, None] >= jnp.arange(SEQ)[None, :]
    scores = jnp.where(allowed[None], scores, -1e+30)
    probs = jax.nn.softmax(scores, axis=-1)
    weights = probs.astype(jnp.bfloat16)
    context = jnp.einsum('hqk,khd->qhd', weights.astype(jnp.float32), keyvals)
    context = context.astype(jnp.bfloat16).reshape(SEQ, -1)
    return (queries, keyvals, probs, weights, context)

def normalize(values, gain_row):
    inverse = lax.rsqrt(lax.optimization_barrier(jnp.sum(values * values, axis=-1)) / D + EPSILON)
    normed = (values * inverse[:, None] * gain_row[None]).astype(jnp.bfloat16)
    return (inverse, normed)

def one_section(items):
    fresh, fetched, grad_rows, gain_row, weight = items
    fresh_f = fresh.astype(jnp.float32)
    inverse_f, normed_f = normalize(fresh_f, gain_row)
    context_f = attend(normed_f)[4]
    output = (fresh_f + jnp.dot(context_f, weight, preferred_element_type=jnp.float32)).astype(jnp.bfloat16)
    held_f = fetched.astype(jnp.float32)
    inverse_b, normed_b = normalize(held_f, gain_row)
    queries, keyvals, probs, weights, unused = attend(normed_b)
    dcontext = jnp.dot(grad_rows, weight.T, preferred_element_type=jnp.float32).astype(jnp.bfloat16)
    dcontext = dcontext.reshape(SEQ, D // (2 * HD), HD).astype(jnp.float32)
    dprob = jnp.einsum('qhd,khd->hqk', dcontext, keyvals)
    dvalue = jnp.einsum('hqk,qhd->khd', weights.astype(jnp.float32), dcontext)
    shrink = HD ** (-0.5)
    dscore = (probs * (dprob - lax.optimization_barrier(jnp.sum(dprob * probs, axis=-1, keepdims=True))) * shrink).astype(jnp.bfloat16)
    dscore = dscore.astype(jnp.float32)
    dquery = jnp.einsum('hqk,khd->qhd', dscore, keyvals)
    dkey = jnp.einsum('hqk,qhd->khd', dscore, queries)
    dnormed = jnp.stack([dquery, dvalue + dkey], axis=2).reshape(SEQ, D)
    scaled = dnormed * gain_row[None]
    moment = lax.optimization_barrier(jnp.sum(scaled * held_f, axis=-1))
    grad_in = grad_rows.astype(jnp.float32) + inverse_b[:, None] * scaled
    grad_in = grad_in - held_f * (inverse_b ** 3 * moment / D)[:, None]
    return (output, grad_in.astype(jnp.bfloat16))

def reference(section_input, stash_held, upstream, norm_gain, out_weight):
    fetched_all = stash_held[::-1]
    section_output, input_grad = lax.map(one_section, (section_input, fetched_all, upstream, norm_gain, out_weight))
    stash_moved = section_input[::-1]
    return (section_output, stash_moved, input_grad)
```

```python
import functools

import jax
import jax.numpy as jnp
import numpy as np
from jax import lax
from jax.experimental import pallas as pl
from jax.experimental.pallas import tpu as pltpu
from jax.sharding import PartitionSpec as P

HD = 128
EPSILON = 1e-05
SHRINK = HD ** (-0.5)
F32 = jnp.float32
BF16 = jnp.bfloat16


def ring_order(mesh):
    count = mesh.shape["fsdp"]
    at = list(mesh.axis_names).index("fsdp")
    line = np.moveaxis(mesh.devices, at, 0).reshape(count, -1)[:, 0]
    coords = [getattr(d, "coords", None) for d in line]
    if any(c is None for c in coords):
        return list(range(count))
    inner = sum(1 for c in coords if c[2] == coords[0][2])
    if count % inner or (inner > 1 and inner % 2):
        return list(range(count))
    outer = count // inner
    if inner == 1 or outer == 1:
        return list(range(count))
    order = [z * inner for z in range(outer)]
    for y in range(inner - 1, 0, -1):
        rows = range(outer - 1, 0, -1) if (inner - 1 - y) % 2 == 0 else range(1, outer)
        order += [z * inner + y for z in rows]
    if inner == 2:
        return order + [1]
    return order + [y for y in range(inner - 1, 0, -1)]


def causal(tokens):
    rows = lax.broadcasted_iota(jnp.int32, (tokens, tokens), 0)
    cols = lax.broadcasted_iota(jnp.int32, (tokens, tokens), 1)
    return rows >= cols


def as_column(row):
    return jnp.broadcast_to(row, (HD, row.shape[1])).T


def as_row(columns):
    return jnp.sum(columns.T, axis=0, keepdims=True)


def dot(a, b, dims):
    return lax.dot_general(a, b, (dims, ((), ())), preferred_element_type=F32)


def squares_kernel(fresh_ref, held_ref, out_ref):
    for slot, ref in enumerate((fresh_ref, held_ref)):
        total = jnp.zeros((ref.shape[0], HD), F32)
        for start in range(0, ref.shape[1], HD):
            part = ref[:, start : start + HD].astype(F32)
            total = total + part * part
        out_ref[slot : slot + 1, :] = as_row(total)


def squares(fresh, held):
    return pl.pallas_call(
        squares_kernel,
        out_shape=jax.ShapeDtypeStruct((2, fresh.shape[0]), F32),
        name="squares",
    )(fresh, held)


def normed_parts(x_ref, gain_ref, inverse):
    parts = []
    for start in (0, HD):
        x = x_ref[:, start : start + HD].astype(F32)
        parts.append((x * inverse * gain_ref[:, start : start + HD]).astype(BF16))
    return parts


def softmax_of(queries, keyvals):
    scores = dot(queries, keyvals, ((1,), (1,))) * SHRINK
    scores = jnp.where(causal(scores.shape[0]), scores, -1e30)
    powers = jnp.exp(scores - jnp.max(scores, axis=-1, keepdims=True))
    return powers / jnp.sum(powers, axis=-1, keepdims=True)


def forward_kernel(width, x_ref, total_ref, gain_ref, out_ref):
    inverse = as_column(lax.rsqrt(total_ref[...] / width + EPSILON))
    queries, keyvals = normed_parts(x_ref, gain_ref, inverse)
    weights = softmax_of(queries, keyvals).astype(BF16)
    out_ref[...] = dot(weights, keyvals, ((1,), (0,))).astype(BF16)


def forward(x, total, gain, width):
    tokens, local = x.shape
    heads = local // (2 * HD)
    return pl.pallas_call(
        functools.partial(forward_kernel, width),
        grid=(heads,),
        in_specs=[
            pl.BlockSpec((tokens, 2 * HD), lambda h: (0, h)),
            pl.BlockSpec((1, tokens), lambda h: (0, 0)),
            pl.BlockSpec((1, 2 * HD), lambda h: (0, h)),
        ],
        out_specs=pl.BlockSpec((tokens, HD), lambda h: (0, h)),
        out_shape=jax.ShapeDtypeStruct((tokens, local // 2), BF16),
        name="forward",
    )(x, total, gain)


def backward_kernel(width, parts, x_ref, total_ref, gain_ref, *refs):
    grad_refs, (scaled_ref, moment_ref, sums_ref) = refs[:parts], refs[parts:]
    head = pl.program_id(0)
    inverse = as_column(lax.rsqrt(total_ref[...] / width + EPSILON))
    queries, keyvals = normed_parts(x_ref, gain_ref, inverse)
    probs = softmax_of(queries, keyvals)
    grad = grad_refs[0][...]
    for ref in grad_refs[1:]:
        grad = grad + ref[...].astype(F32)
    grad = grad.astype(BF16)
    dprob = dot(grad, keyvals, ((1,), (1,)))
    dvalue = dot(probs.astype(BF16), grad, ((0,), (0,)))
    inner = jnp.sum(dprob * probs, axis=-1, keepdims=True)
    dscore = (probs * (dprob - inner) * SHRINK).astype(BF16)
    dquery = dot(dscore, keyvals, ((1,), (0,)))
    dkeyval = dvalue + dot(dscore, queries, ((0,), (0,)))
    sums = jnp.zeros((x_ref.shape[0], HD), F32)
    for start, value in ((0, dquery), (HD, dkeyval)):
        scaled = value * gain_ref[:, start : start + HD]
        scaled_ref[:, start : start + HD] = scaled
        sums = sums + scaled * x_ref[:, start : start + HD].astype(F32)

    @pl.when(head == 0)
    def _():
        sums_ref[...] = sums

    @pl.when(head > 0)
    def _():
        sums_ref[...] += sums

    @pl.when(head == pl.num_programs(0) - 1)
    def _():
        moment_ref[...] = as_row(sums_ref[...])


def backward(x, total, gain, grads, width):
    tokens, local = x.shape
    heads = local // (2 * HD)
    return pl.pallas_call(
        functools.partial(backward_kernel, width, len(grads)),
        grid=(heads,),
        in_specs=[
            pl.BlockSpec((tokens, 2 * HD), lambda h: (0, h)),
            pl.BlockSpec((1, tokens), lambda h: (0, 0)),
            pl.BlockSpec((1, 2 * HD), lambda h: (0, h)),
        ]
        + [pl.BlockSpec((tokens, HD), lambda h: (0, h)) for _ in grads],
        out_specs=(
            pl.BlockSpec((tokens, 2 * HD), lambda h: (0, h)),
            pl.BlockSpec((1, tokens), lambda h: (0, 0)),
        ),
        out_shape=(
            jax.ShapeDtypeStruct((tokens, local), F32),
            jax.ShapeDtypeStruct((1, tokens), F32),
        ),
        scratch_shapes=[pltpu.VMEM((tokens, HD), F32)],
        name="backward",
    )(x, total, gain, *grads)


def finish_kernel(width, rows_ref, x_ref, scaled_ref, total_ref, moment_ref, out_ref):
    inverse = lax.rsqrt(total_ref[...] / width + EPSILON)
    pull = as_column(inverse**3 * moment_ref[...] / width)
    inverse = as_column(inverse)
    for start in range(0, rows_ref.shape[1], HD):
        at = slice(start, start + HD)
        grad = rows_ref[:, at].astype(F32) + inverse * scaled_ref[:, at]
        out_ref[:, at] = (grad - x_ref[:, at].astype(F32) * pull).astype(BF16)


def finish(rows, x, scaled, total, moment, width):
    tokens, local = rows.shape
    block = pl.BlockSpec((tokens, 2 * HD), lambda h: (0, h))
    whole = pl.BlockSpec((1, tokens), lambda h: (0, 0))
    return pl.pallas_call(
        functools.partial(finish_kernel, width),
        grid=(local // (2 * HD),),
        in_specs=[block, block, block, whole, whole],
        out_specs=block,
        out_shape=jax.ShapeDtypeStruct((tokens, local), BF16),
        name="finish",
    )(rows, x, scaled, total, moment)


def piece(size, most):
    fits = [p for p in range(128, min(size, most) + 1, 128) if size % p == 0]
    return fits[-1] if fits else size


def partial_kernel(ids_ref, rows_ref, weight_ref, out_ref):
    out_ref[0] = dot(rows_ref[...], weight_ref[...], ((1,), (1,)))


def partial_sums(ids, rows, weight, first, count, chunk):
    tokens, depth = rows.shape
    block = piece(chunk, 384)
    pieces = chunk // block
    return pl.pallas_call(
        partial_kernel,
        grid_spec=pltpu.PrefetchScalarGridSpec(
            num_scalar_prefetch=1,
            grid=(count, pieces),
            in_specs=[
                pl.BlockSpec((tokens, depth), lambda c, j, ids: (0, 0)),
                pl.BlockSpec((block, depth), lambda c, j, ids: (ids[first + c] * pieces + j, 0)),
            ],
            out_specs=pl.BlockSpec((1, tokens, block), lambda c, j, ids: (c, 0, j)),
        ),
        out_shape=jax.ShapeDtypeStruct((count, tokens, chunk), F32),
        name="partial",
    )(ids, rows, weight)


def project_kernel(base_kind, split, ids_ref, *refs):
    refs = list(refs)
    out_ref = refs.pop()
    base = refs.pop(0)[...] if base_kind else None
    extra = refs.pop(0)[...] if base_kind == "last" else None
    weights = refs[-1:] if split else refs[len(refs) // 2 :]
    if split:
        total = jnp.concatenate(
            [dot(half[...], weights[0][...], ((1,), (0,))) for half in refs[:-1]], axis=0
        )
    else:
        total = None
        for context, weight in zip(refs[: len(refs) // 2], weights):
            term = dot(context[...], weight[...], ((1,), (0,)))
            total = term if total is None else total + term
    if base is not None:
        total = base + total
    if extra is not None:
        total = extra.astype(F32) + total
    out_ref[...] = total.astype(out_ref.dtype)


def project(ids, weight, contexts, slots, base=None, extra=None, split=False):
    chunk = contexts[0].shape[1]
    tokens = sum(c.shape[0] for c in contexts) if split else contexts[0].shape[0]
    width = weight.shape[1]
    block = piece(width, 512)
    column = pl.BlockSpec((tokens, block), lambda j, ids: (0, j))
    operands, specs = [], []
    if base is not None:
        operands.append(base)
        specs.append(column)
    if extra is not None:
        operands.append(extra)
        specs.append(column)
    for c in contexts:
        operands.append(c)
        specs.append(pl.BlockSpec(c.shape, lambda j, ids: (0, 0)))
    for slot in slots:
        operands.append(weight)
        specs.append(pl.BlockSpec((chunk, block), lambda j, ids, slot=slot: (ids[slot], j)))
    kind = None if base is None else ("last" if extra is not None else "sum")
    return pl.pallas_call(
        functools.partial(project_kernel, kind, split),
        grid_spec=pltpu.PrefetchScalarGridSpec(
            num_scalar_prefetch=1,
            grid=(width // block,),
            in_specs=specs,
            out_specs=column,
        ),
        out_shape=jax.ShapeDtypeStruct((tokens, width), BF16 if extra is not None else F32),
        name="project",
    )(ids, *operands)


def mirrored(value):
    sections = lax.axis_size("section")
    return lax.ppermute(value, "section", [(i, sections - 1 - i) for i in range(sections)])


def total_over(value, axis):
    size = lax.axis_size(axis)
    stride = 1
    while stride < size:
        factor = next(f for f in range(2, size + 1) if (size // stride) % f == 0)
        terms = [value]
        for turn in range(1, factor):
            pairs = []
            for i in range(size):
                digit = (i // stride) % factor
                pairs.append((i, i + ((digit + turn) % factor - digit) * stride))
            terms.append(lax.ppermute(value, axis, pairs))
        value = functools.reduce(jnp.add, terms)
        stride *= factor
    return value


def local(order, section_input, stash_held, upstream, norm_gain, out_weight):
    fresh, held, rows = section_input[0], stash_held[0], upstream[0]
    gain, weight = norm_gain, out_weight[0]
    count = len(order)
    tokens = fresh.shape[0]
    width = fresh.shape[1] * count
    chunk = weight.shape[0] // count
    half = tokens // 2
    far = (count - 1) // 2
    opposite = count % 2 == 0

    def turn(value, step):
        return lax.ppermute(
            value, "fsdp", [(order[i], order[(i + step) % count]) for i in range(count)]
        )

    offsets = [count // 2] if opposite else []
    for distance in range(far, 0, -1):
        offsets += [distance, -distance]
    offsets.append(0)
    slot_of = {offset: slot for slot, offset in enumerate(offsets)}
    table = np.zeros((count, len(offsets)), np.int32)
    for at, device in enumerate(order):
        table[device] = [order[(at + offset) % count] for offset in offsets]
    ids = jnp.asarray(table)[lax.axis_index("fsdp")]

    fetched = mirrored(held)
    sums = squares(fresh, held)

    up = down = None
    if opposite:
        first = partial_sums(ids, rows, weight, slot_of[count // 2], 1, chunk)[0].astype(BF16)
        if count > 2:
            up, down = turn(first[:half], 1), turn(first[half:], -1)
        else:
            up, down = turn(first[:half], 1), turn(first[half:], 1)
    narrow = opposite
    for distance in range(far, 0, -1):
        both = partial_sums(ids, rows, weight, slot_of[distance], 2, chunk)
        ahead, behind = both[0], both[1]
        if narrow:
            ahead = jnp.concatenate([ahead[:half] + up.astype(F32), ahead[half:]])
            behind = jnp.concatenate([behind[:half], behind[half:] + down.astype(F32)])
        elif up is not None:
            ahead, behind = ahead + up.astype(F32), behind + down.astype(F32)
        narrow = False
        up, down = turn(ahead.astype(BF16), 1), turn(behind.astype(BF16), -1)
    own = partial_sums(ids, rows, weight, slot_of[0], 1, chunk)[0]
    if narrow:
        grads = [own, jnp.concatenate([up, down])]
    elif up is not None:
        grads = [own, up, down]
    else:
        grads = [own]

    totals = total_over(sums, "fsdp")
    total_b = mirrored(totals[1:2])
    context = forward(fresh, totals[0:1], gain, width)

    projected = None
    up = down = context
    arrived, slots = [context], [slot_of[0]]
    for distance in range(1, far + 1):
        up, down = turn(up, 1), turn(down, -1)
        arrived += [up, down]
        slots += [slot_of[-distance], slot_of[distance]]
        if distance < far or opposite:
            projected = project(ids, weight, arrived, slots, projected)
            arrived, slots = [], []
    if opposite:
        if count > 2:
            up, down = turn(up[:half], 1), turn(down[half:], -1)
        else:
            projected = project(ids, weight, arrived, slots, projected)
            up, down = turn(up[:half], 1), turn(down[half:], 1)
        output = project(
            ids, weight, [up, down], [slot_of[count // 2]], projected, fresh, split=True
        )
    else:
        if projected is None:
            projected = jnp.zeros(fresh.shape, F32)
        output = project(ids, weight, arrived, slots, projected, fresh)

    scaled, moment = backward(fetched, total_b, gain, grads, width)
    moment = total_over(moment, "fsdp")
    grad_in = finish(rows, fetched, scaled, total_b, moment, width)
    parked = mirrored(fresh)
    return (output[None], parked[None], grad_in[None])


def solution(mesh):
    order = ring_order(mesh)
    placed = P("section", None, "fsdp")
    return jax.shard_map(
        functools.partial(local, order),
        mesh=mesh,
        in_specs=(placed, placed, placed, P("section", "fsdp"), placed),
        out_specs=(placed, placed, placed),
        check_vma=False,
    )
```

```python
import functools

import jax
import jax.numpy as jnp
import numpy as np
from jax import lax
from jax.experimental import pallas as pl
from jax.experimental.pallas import tpu as pltpu
from jax.sharding import PartitionSpec as P

HD = 128
EPSILON = 1e-05
SHRINK = HD ** (-0.5)
F32 = jnp.float32
BF16 = jnp.bfloat16


def ring_order(mesh):
    count = mesh.shape["fsdp"]
    at = list(mesh.axis_names).index("fsdp")
    line = np.moveaxis(mesh.devices, at, 0).reshape(count, -1)[:, 0]
    coords = [getattr(d, "coords", None) for d in line]
    if any(c is None for c in coords):
        return list(range(count))
    inner = sum(1 for c in coords if c[2] == coords[0][2])
    if count % inner or (inner > 1 and inner % 2):
        return list(range(count))
    outer = count // inner
    if inner == 1 or outer == 1:
        return list(range(count))
    order = [z * inner for z in range(outer)]
    for y in range(inner - 1, 0, -1):
        rows = range(outer - 1, 0, -1) if (inner - 1 - y) % 2 == 0 else range(1, outer)
        order += [z * inner + y for z in rows]
    if inner == 2:
        return order + [1]
    return order + [y for y in range(inner - 1, 0, -1)]


VMEM = pl.BlockSpec(memory_space=pltpu.VMEM)
ANY = pl.BlockSpec(memory_space=pl.ANY)
ROOM = 12 * 2**20


def run(kernel, operands, results, after=(), room=ROOM):
    def body(*refs):
        kernel(*refs[: len(operands)], *refs[len(operands) + len(after) :])

    return pl.pallas_call(
        body,
        in_specs=[VMEM] * (len(operands) + len(after)),
        out_specs=[VMEM] * len(results),
        out_shape=[pltpu.VMEM(shape, kind) for shape, kind in results],
        compiler_params=pltpu.CompilerParams(vmem_limit_bytes=room),
    )(*operands, *after)


def causal(tokens):
    rows = lax.broadcasted_iota(jnp.int32, (tokens, tokens), 0)
    cols = lax.broadcasted_iota(jnp.int32, (tokens, tokens), 1)
    return rows >= cols


def as_column(row):
    return jnp.broadcast_to(row, (HD, row.shape[1])).T


def as_row(columns):
    return jnp.sum(columns.T, axis=0, keepdims=True)


def dot(a, b, dims):
    return lax.dot_general(a, b, (dims, ((), ())), preferred_element_type=F32)


def first_row(plan, offset, chunk):
    me = lax.axis_index("fsdp")
    row = jnp.int32(0)
    for device, owner in enumerate(plan[offset]):
        row = jnp.where(me == device, owner * chunk, row)
    return pl.multiple_of(row, chunk)


def begin(plan, fresh, held, rows, weight, chunk, opposite):
    tokens, depth = rows.shape
    count = len(plan[0])

    def body(fresh_ref, held_ref, rows_ref, weight_ref, *rest):
        outs, (fresh_v, held_v, rows_v, weight_v, sems) = rest[:-5], rest[-5:]
        copies = [
            pltpu.make_async_copy(fresh_ref, fresh_v, sems.at[2]),
            pltpu.make_async_copy(held_ref, held_v, sems.at[3]),
        ]
        if opposite:
            at = first_row(plan, count // 2, chunk)
            near = [
                pltpu.make_async_copy(rows_ref, rows_v, sems.at[0]),
                pltpu.make_async_copy(weight_ref.at[pl.ds(at, chunk), :], weight_v, sems.at[1]),
            ]
            for copy in near:
                copy.start()
        for copy in copies:
            copy.start()
        for slot, (copy, ref) in enumerate(zip(copies, (fresh_v, held_v))):
            copy.wait()
            total = jnp.zeros((tokens, HD), F32)
            for start in range(0, depth, HD):
                part = ref[:, start : start + HD].astype(F32)
                total = total + part * part
            outs[0][slot : slot + 1, :] = as_row(total)
        if opposite:
            for copy in near:
                copy.wait()
            for out, start in zip(outs[1:], (0, tokens // 2)):
                part = rows_v[start : start + tokens // 2, :]
                out[...] = dot(part, weight_v[...], ((1,), (1,))).astype(BF16)

    results = [((2, tokens), F32)]
    if opposite:
        results += [((tokens // 2, chunk), BF16)] * 2
    return pl.pallas_call(
        body,
        in_specs=[ANY] * 4,
        out_specs=[VMEM] * len(results),
        out_shape=[pltpu.VMEM(shape, kind) for shape, kind in results],
        scratch_shapes=[
            pltpu.VMEM((tokens, depth), BF16),
            pltpu.VMEM((tokens, depth), BF16),
            pltpu.VMEM((tokens, depth), BF16),
            pltpu.VMEM((chunk, depth), BF16),
            pltpu.SemaphoreType.DMA((4,)),
        ],
        compiler_params=pltpu.CompilerParams(vmem_limit_bytes=ROOM),
        name="begin",
    )(fresh, held, rows, weight)


def partial_sums(plan, rows, weight, offsets, chunk, after):
    def kernel(rows_ref, weight_ref, *outs):
        for offset, out in zip(offsets, outs):
            at = first_row(plan, offset, chunk)
            out[...] = dot(rows_ref[...], weight_ref[pl.ds(at, chunk), :], ((1,), (1,)))

    results = [((rows.shape[0], chunk), F32)] * len(offsets)
    return run(kernel, (rows, weight), results, after)


def add_arrived(ahead, behind, up, down, after):
    def kernel(ahead_ref, behind_ref, *refs):
        half = ahead_ref.shape[0] // 2
        if up is None:
            refs[0][...] = ahead_ref[...].astype(BF16)
            refs[1][...] = behind_ref[...].astype(BF16)
            return
        up_ref, down_ref, to_up, to_down = refs
        if up_ref.shape[0] == half:
            to_up[:half] = (ahead_ref[:half] + up_ref[...].astype(F32)).astype(BF16)
            to_up[half:] = ahead_ref[half:].astype(BF16)
            to_down[:half] = behind_ref[:half].astype(BF16)
            to_down[half:] = (behind_ref[half:] + down_ref[...].astype(F32)).astype(BF16)
        else:
            to_up[...] = (ahead_ref[...] + up_ref[...].astype(F32)).astype(BF16)
            to_down[...] = (behind_ref[...] + down_ref[...].astype(F32)).astype(BF16)

    operands = (ahead, behind) + (() if up is None else (up, down))
    return run(kernel, operands, [(ahead.shape, BF16)] * 2, after)


def normed_parts(x_ref, gain_ref, inverse, head):
    parts = []
    for start in (head * 2 * HD, head * 2 * HD + HD):
        x = x_ref[:, start : start + HD].astype(F32)
        parts.append((x * inverse * gain_ref[:, start : start + HD]).astype(BF16))
    return parts


def softmax_of(queries, keyvals):
    scores = dot(queries, keyvals, ((1,), (1,))) * SHRINK
    scores = jnp.where(causal(scores.shape[0]), scores, -1e30)
    powers = jnp.exp(scores - jnp.max(scores, axis=-1, keepdims=True))
    return powers / jnp.sum(powers, axis=-1, keepdims=True)


def forward(x, totals, gain, width, after):
    tokens, depth = x.shape

    def kernel(x_ref, gain_ref, *refs):
        total = refs[0][0:1, :]
        for ref in refs[1:-1]:
            total = total + ref[0:1, :]
        inverse = as_column(lax.rsqrt(total / width + EPSILON))
        for head in range(depth // (2 * HD)):
            queries, keyvals = normed_parts(x_ref, gain_ref, inverse, head)
            weights = softmax_of(queries, keyvals).astype(BF16)
            out = dot(weights, keyvals, ((1,), (0,))).astype(BF16)
            refs[-1][:, head * HD : (head + 1) * HD] = out

    return run(kernel, (x, gain, *totals), [((tokens, depth // 2), BF16)], after)[0]


def prepare(x, total, gain, width, after):
    tokens, depth = x.shape
    heads = depth // (2 * HD)

    def kernel(x_ref, total_ref, gain_ref, queries_ref, keyvals_ref, probs_ref):
        inverse = as_column(lax.rsqrt(total_ref[...] / width + EPSILON))
        for head in range(heads):
            queries, keyvals = normed_parts(x_ref, gain_ref, inverse, head)
            at = slice(head * HD, (head + 1) * HD)
            queries_ref[:, at] = queries
            keyvals_ref[:, at] = keyvals
            probs_ref[head] = softmax_of(queries, keyvals)

    results = [((tokens, depth // 2), BF16)] * 2 + [((heads, tokens, tokens), F32)]
    return run(kernel, (x, total, gain), results, after)


def backward(x, gain, queries, keyvals, probs, grads, after):
    tokens, depth = x.shape

    def kernel(x_ref, gain_ref, queries_ref, keyvals_ref, probs_ref, *refs):
        grad_refs, (scaled_ref, moment_ref) = refs[:-2], refs[-2:]
        sums = jnp.zeros((tokens, HD), F32)
        half = tokens // 2
        for head in range(depth // (2 * HD)):
            at = slice(head * HD, (head + 1) * HD)
            queries, keyvals, probs = queries_ref[:, at], keyvals_ref[:, at], probs_ref[head]
            grad = grad_refs[0][:, at]
            if len(grad_refs) > 1 and grad_refs[1].shape[0] == half:
                arrived = jnp.concatenate([ref[:, at] for ref in grad_refs[1:]], axis=0)
                grad = grad + arrived.astype(F32)
            else:
                for ref in grad_refs[1:]:
                    grad = grad + ref[:, at].astype(F32)
            grad = grad.astype(BF16)
            dprob = dot(grad, keyvals, ((1,), (1,)))
            dvalue = dot(probs.astype(BF16), grad, ((0,), (0,)))
            inner = jnp.sum(dprob * probs, axis=-1, keepdims=True)
            dscore = (probs * (dprob - inner) * SHRINK).astype(BF16)
            dquery = dot(dscore, keyvals, ((1,), (0,)))
            dkeyval = dvalue + dot(dscore, queries, ((0,), (0,)))
            for start, value in ((0, dquery), (HD, dkeyval)):
                to = slice(head * 2 * HD + start, head * 2 * HD + start + HD)
                scaled = value * gain_ref[:, to]
                scaled_ref[:, to] = scaled
                sums = sums + scaled * x_ref[:, to].astype(F32)
        moment_ref[...] = as_row(sums)

    results = [((tokens, depth), F32), ((1, tokens), F32)]
    return run(kernel, (x, gain, queries, keyvals, probs, *grads), results, after)


def finish(rows, x, scaled, total, moments, width, after):
    tokens, depth = rows.shape

    def kernel(rows_ref, x_ref, scaled_ref, total_ref, *refs):
        moment = refs[0][...]
        for ref in refs[1:-1]:
            moment = moment + ref[...]
        inverse = lax.rsqrt(total_ref[...] / width + EPSILON)
        pull = as_column(inverse**3 * moment / width)
        inverse = as_column(inverse)
        for start in range(0, depth, HD):
            at = slice(start, start + HD)
            grad = rows_ref[:, at].astype(F32) + inverse * scaled_ref[:, at]
            refs[-1][:, at] = (grad - x_ref[:, at].astype(F32) * pull).astype(BF16)

    operands = (rows, x, scaled, total, *moments)
    return run(kernel, operands, [((tokens, depth), BF16)], after)[0]


def piece(size, most):
    fits = [p for p in range(128, min(size, most) + 1, 128) if size % p == 0]
    return fits[-1] if fits else size


def project(plan, weight, contexts, offsets, chunk, base, after):
    tokens, width = contexts[0].shape[0], weight.shape[1]

    def kernel(weight_ref, *refs):
        total = None
        for context, offset in zip(refs, offsets):
            at = first_row(plan, offset, chunk)
            term = dot(context[...], weight_ref[pl.ds(at, chunk), :], ((1,), (0,)))
            total = term if total is None else total + term
        if base is not None:
            total = refs[len(offsets)][...] + total
        refs[-1][...] = total

    operands = (weight, *contexts) + (() if base is None else (base,))
    return run(kernel, operands, [((tokens, width), F32)], after)[0]


def project_last(plan, weight, contexts, offsets, chunk, base, fresh, after):
    tokens, width = fresh.shape
    block = piece(width, 512)
    halves = contexts[0].shape[0] != tokens

    def body(weight_ref, base_ref, fresh_ref, *refs):
        parts, (out_ref, held_ref, sems) = refs[: len(contexts)], refs[-3:]
        copies = []
        for turn, start in enumerate(range(0, width, block)):
            cols = slice(start, start + block)
            if halves:
                at = first_row(plan, offsets[0], chunk)
                weights = weight_ref[pl.ds(at, chunk), cols]
                total = jnp.concatenate([dot(p[...], weights, ((1,), (0,))) for p in parts], axis=0)
            else:
                total = jnp.zeros((tokens, block), F32)
                for context, offset in zip(parts, offsets):
                    at = first_row(plan, offset, chunk)
                    total += dot(context[...], weight_ref[pl.ds(at, chunk), cols], ((1,), (0,)))
            total = fresh_ref[:, cols].astype(F32) + (base_ref[:, cols] + total)
            held_ref[:, cols] = total.astype(BF16)
            copy = pltpu.make_async_copy(held_ref.at[:, cols], out_ref.at[:, cols], sems.at[turn])
            copy.start()
            copies.append(copy)
        for copy in copies:
            copy.wait()

    return pl.pallas_call(
        body,
        in_specs=[VMEM] * (3 + len(contexts) + len(after)),
        out_specs=ANY,
        out_shape=jax.ShapeDtypeStruct((tokens, width), BF16),
        scratch_shapes=[
            pltpu.VMEM((tokens, width), BF16),
            pltpu.SemaphoreType.DMA((width // block,)),
        ],
        compiler_params=pltpu.CompilerParams(vmem_limit_bytes=ROOM),
        name="last",
    )(weight, base, fresh, *contexts, *after)


def mirrored(value):
    sections = lax.axis_size("section")
    return lax.ppermute(value, "section", [(i, sections - 1 - i) for i in range(sections)])


def stages(size):
    stride, found = 1, []
    while stride < size:
        factor = next(f for f in range(2, size + 1) if (size // stride) % f == 0)
        found.append((stride, factor))
        stride *= factor
    return found


def exchanged(value, stage, size):
    stride, factor = stage
    terms = [value]
    for turn in range(1, factor):
        pairs = []
        for i in range(size):
            digit = (i // stride) % factor
            pairs.append((i, i + ((digit + turn) % factor - digit) * stride))
        terms.append(lax.ppermute(value, "fsdp", pairs))
    return terms


def local(order, section_input, stash_held, upstream, norm_gain, out_weight):
    fresh, held, rows = section_input[0], stash_held[0], upstream[0]
    gain, weight = norm_gain, out_weight[0]
    count = len(order)
    tokens = fresh.shape[0]
    width = fresh.shape[1] * count
    chunk = weight.shape[0] // count
    half = tokens // 2
    far = (count - 1) // 2
    opposite = count % 2 == 0
    place = {device: at for at, device in enumerate(order)}
    plan = {
        offset: [order[(place[device] + offset) % count] for device in range(count)]
        for offset in range(-far, count // 2 + 1)
    }
    steps = stages(count)

    def turn(value, step):
        pairs = [(order[i], order[(i + step) % count]) for i in range(count)]
        return lax.ppermute(value, "fsdp", pairs)

    sums, *first = begin(plan, fresh, held, rows, weight, chunk, opposite)
    fetched = mirrored(held)
    up = down = None
    if opposite:
        up = turn(first[0], 1)
        down = turn(first[1], -1 if count > 2 else 1)

    terms = [sums]
    for stage in steps:
        terms = exchanged(functools.reduce(jnp.add, terms), stage, count)
    total_b = mirrored(functools.reduce(jnp.add, [t[1:2] for t in terms]))

    last, context = sums, None
    for distance in range(far, 0, -1):
        pair = partial_sums(plan, rows, weight, (distance, -distance), chunk, (last,))
        last = pair[0]
        if distance == max(far - 1, 1):
            context = forward(fresh, terms, gain, width, (last,))
            last = context
        if distance == 1:
            own = partial_sums(plan, rows, weight, (0,), chunk, (last,))[0]
            last = own
        to_up, to_down = add_arrived(*pair, up, down, (last,))
        last = to_up
        up = turn(to_up, 1)
        down = turn(to_down, -1)
    if far == 0:
        own = partial_sums(plan, rows, weight, (0,), chunk, (last,))[0]
        context = forward(fresh, terms, gain, width, (own,))
    grads = [own] if up is None else [own, up, down]

    queries, keyvals, probs = prepare(fetched, total_b, gain, width, (last,))
    last = queries
    projected = None
    ahead = behind = context
    arrived, offsets = [context], [0]
    scaled = None
    for distance in range(1, far + 1):
        ahead, behind = turn(ahead, 1), turn(behind, -1)
        arrived += [ahead, behind]
        offsets += [-distance, distance]
        if distance < far or opposite:
            projected = project(plan, weight, arrived, offsets, chunk, projected, (last,))
            last = projected
            arrived, offsets = [], []
        if scaled is None:
            scaled, moment = backward(
                fetched, gain, queries, keyvals, probs, grads, (last,)
            )
            last = scaled
    if scaled is None:
        scaled, moment = backward(fetched, gain, queries, keyvals, probs, grads, (last,))
    moments = [moment]
    for stage in steps:
        moments = exchanged(functools.reduce(jnp.add, moments), stage, count)
    grad_in = finish(rows, fetched, scaled, total_b, moments, width, ())
    if projected is None:
        if arrived:
            projected = project(plan, weight, arrived, offsets, chunk, None, ())
            arrived, offsets = [], []
    if opposite:
        ahead = turn(ahead[:half], 1)
        behind = turn(behind[half:], -1 if count > 2 else 1)
        arrived, offsets = [ahead, behind], [count // 2]
    output = project_last(plan, weight, arrived, offsets, chunk, projected, fresh, (grad_in,))
    parked = mirrored(fresh)
    return (output[None], parked[None], grad_in[None])


def solution(mesh):
    order = ring_order(mesh)
    placed = P("section", None, "fsdp")

    def body(*arrays):
        return local(order, *arrays)

    return jax.shard_map(
        body,
        mesh=mesh,
        in_specs=(placed, placed, placed, P("section", "fsdp"), placed),
        out_specs=(placed, placed, placed),
        check_vma=False,
    )
```

```python
import functools

import jax
import jax.numpy as jnp
import numpy as np
from jax import lax
from jax.experimental import pallas as pl
from jax.experimental.pallas import tpu as pltpu
from jax.sharding import PartitionSpec as P

HD = 128
EPSILON = 1e-05
NARROW = (2, 3, 5)
WIDE = (4, 2, 3, 5)
SHRINK = HD ** (-0.5)
F32 = jnp.float32
BF16 = jnp.bfloat16


def ring_order(mesh):
    count = mesh.shape["fsdp"]
    at = list(mesh.axis_names).index("fsdp")
    line = np.moveaxis(mesh.devices, at, 0).reshape(count, -1)[:, 0]
    coords = [getattr(d, "coords", None) for d in line]
    if any(c is None for c in coords):
        return list(range(count))
    inner = sum(1 for c in coords if c[2] == coords[0][2])
    if count % inner or (inner > 1 and inner % 2):
        return list(range(count))
    outer = count // inner
    if inner == 1 or outer == 1:
        return list(range(count))
    order = [z * inner for z in range(outer)]
    for y in range(inner - 1, 0, -1):
        rows = range(outer - 1, 0, -1) if (inner - 1 - y) % 2 == 0 else range(1, outer)
        order += [z * inner + y for z in rows]
    if inner == 2:
        return order + [1]
    return order + [y for y in range(inner - 1, 0, -1)]


VMEM = pl.BlockSpec(memory_space=pltpu.VMEM)
HBM = pl.BlockSpec(memory_space=pltpu.HBM)
ROOM = 12 * 2**20


def run(kernel, operands, results, after=(), room=ROOM):
    def body(*refs):
        kernel(*refs[: len(operands)], *refs[len(operands) + len(after) :])

    return pl.pallas_call(
        body,
        in_specs=[VMEM] * (len(operands) + len(after)),
        out_specs=[VMEM] * len(results),
        out_shape=[pltpu.VMEM(shape, kind) for shape, kind in results],
        compiler_params=pltpu.CompilerParams(vmem_limit_bytes=room),
    )(*operands, *after)


def causal(tokens):
    rows = lax.broadcasted_iota(jnp.int32, (tokens, tokens), 0)
    cols = lax.broadcasted_iota(jnp.int32, (tokens, tokens), 1)
    return rows >= cols


def as_column(row):
    return jnp.broadcast_to(row, (HD, row.shape[1])).T


def as_row(columns):
    return jnp.sum(columns.T, axis=0, keepdims=True)


def dot(a, b, dims):
    return lax.dot_general(a, b, (dims, ((), ())), preferred_element_type=F32)


def first_row(plan, offset, chunk):
    me = lax.axis_index("fsdp")
    row = jnp.int32(0)
    for device, owner in enumerate(plan[offset]):
        row = jnp.where(me == device, owner * chunk, row)
    return pl.multiple_of(row, chunk)


def squares(fresh, held):
    tokens, depth = fresh.shape[1:]

    def body(fresh_ref, held_ref, out_ref, fresh_v, held_v, sems):
        copies = []
        for slot, (ref, to) in enumerate(((fresh_ref, fresh_v), (held_ref, held_v))):
            copies.append(pltpu.make_async_copy(ref.at[0], to, sems.at[slot]))
            copies[-1].start()
        for slot, (copy, ref) in enumerate(zip(copies, (fresh_v, held_v))):
            copy.wait()
            total = jnp.zeros((tokens, HD), F32)
            for start in range(0, depth, HD):
                part = ref[:, start : start + HD].astype(F32)
                total = total + part * part
            out_ref[slot : slot + 1, :] = as_row(total)

    return pl.pallas_call(
        body,
        in_specs=[HBM] * 2,
        out_specs=VMEM,
        out_shape=pltpu.VMEM((2, tokens), F32),
        scratch_shapes=[
            pltpu.VMEM((tokens, depth), BF16),
            pltpu.VMEM((tokens, depth), BF16),
            pltpu.SemaphoreType.DMA((2,)),
        ],
        compiler_params=pltpu.CompilerParams(vmem_limit_bytes=ROOM),
        name="squares",
    )(*(pltpu.with_memory_space_constraint(a, pltpu.HBM) for a in (fresh, held)))


def first_halves(plan, rows, weight, offset, chunk, after):
    tokens, depth = rows.shape[1:]
    half = tokens // 2
    block = piece(chunk, 384)
    pieces = chunk // block

    def body(rows_ref, weight_ref, *refs):
        up_ref, down_ref, rows_v, weight_v, sems = refs[len(after) :]
        at = first_row(plan, offset, chunk)
        copies = [pltpu.make_async_copy(rows_ref.at[0], rows_v, sems.at[0])]
        for turn in range(pieces):
            source = weight_ref.at[0, pl.ds(at + turn * block, block), :]
            to = weight_v.at[pl.ds(turn * block, block), :]
            copies.append(pltpu.make_async_copy(source, to, sems.at[1 + turn]))
        for copy in copies:
            copy.start()
        copies[0].wait()
        for turn in range(pieces):
            copies[1 + turn].wait()
            cols = slice(turn * block, (turn + 1) * block)
            part = dot(rows_v[...], weight_v[cols, :], ((1,), (1,))).astype(BF16)
            up_ref[:, cols] = part[:half]
            down_ref[:, cols] = part[half:]

    return pl.pallas_call(
        body,
        in_specs=[HBM] * 2 + [VMEM] * len(after),
        out_specs=[VMEM] * 2,
        out_shape=[pltpu.VMEM((half, chunk), BF16)] * 2,
        scratch_shapes=[
            pltpu.VMEM((tokens, depth), BF16),
            pltpu.VMEM((chunk, depth), BF16),
            pltpu.SemaphoreType.DMA((1 + pieces,)),
        ],
        compiler_params=pltpu.CompilerParams(vmem_limit_bytes=ROOM),
        name="halves",
    )(*(pltpu.with_memory_space_constraint(a, pltpu.HBM) for a in (rows, weight)), *after)


def partial_sums(plan, rows, weight, offsets, chunk, after):
    def kernel(rows_ref, weight_ref, *outs):
        for offset, out in zip(offsets, outs):
            at = first_row(plan, offset, chunk)
            out[...] = dot(rows_ref[...], weight_ref[pl.ds(at, chunk), :], ((1,), (1,)))

    results = [((rows.shape[0], chunk), F32)] * len(offsets)
    return run(kernel, (rows, weight), results, after)


def add_arrived(ahead, behind, up, down, after):
    def kernel(ahead_ref, behind_ref, *refs):
        half = ahead_ref.shape[0] // 2
        if up is None:
            refs[0][...] = ahead_ref[...].astype(BF16)
            refs[1][...] = behind_ref[...].astype(BF16)
            return
        up_ref, down_ref, to_up, to_down = refs
        if up_ref.shape[0] == half:
            to_up[:half] = (ahead_ref[:half] + up_ref[...].astype(F32)).astype(BF16)
            to_up[half:] = ahead_ref[half:].astype(BF16)
            to_down[:half] = behind_ref[:half].astype(BF16)
            to_down[half:] = (behind_ref[half:] + down_ref[...].astype(F32)).astype(BF16)
        else:
            to_up[...] = (ahead_ref[...] + up_ref[...].astype(F32)).astype(BF16)
            to_down[...] = (behind_ref[...] + down_ref[...].astype(F32)).astype(BF16)

    operands = (ahead, behind) + (() if up is None else (up, down))
    return run(kernel, operands, [(ahead.shape, BF16)] * 2, after)


def normed_parts(x_ref, gain_ref, inverse, head):
    parts = []
    for start in (head * 2 * HD, head * 2 * HD + HD):
        x = x_ref[:, start : start + HD].astype(F32)
        parts.append((x * inverse * gain_ref[:, start : start + HD]).astype(BF16))
    return parts


def softmax_of(queries, keyvals):
    scores = dot(queries, keyvals, ((1,), (1,))) * SHRINK
    scores = jnp.where(causal(scores.shape[0]), scores, -1e30)
    powers = jnp.exp(scores - jnp.max(scores, axis=-1, keepdims=True))
    return powers / jnp.sum(powers, axis=-1, keepdims=True)


def forward(x, totals, gain, width, after):
    tokens, depth = x.shape

    def kernel(x_ref, gain_ref, *refs):
        total = refs[0][0:1, :]
        for ref in refs[1:-1]:
            total = total + ref[0:1, :]
        inverse = as_column(lax.rsqrt(total / width + EPSILON))
        for head in range(depth // (2 * HD)):
            queries, keyvals = normed_parts(x_ref, gain_ref, inverse, head)
            weights = softmax_of(queries, keyvals).astype(BF16)
            out = dot(weights, keyvals, ((1,), (0,))).astype(BF16)
            refs[-1][:, head * HD : (head + 1) * HD] = out

    return run(kernel, (x, gain, *totals), [((tokens, depth // 2), BF16)], after)[0]


def prepare(x, total, gain, width, after):
    tokens, depth = x.shape
    heads = depth // (2 * HD)

    def kernel(x_ref, total_ref, gain_ref, queries_ref, keyvals_ref, probs_ref):
        inverse = as_column(lax.rsqrt(total_ref[...] / width + EPSILON))
        for head in range(heads):
            queries, keyvals = normed_parts(x_ref, gain_ref, inverse, head)
            at = slice(head * HD, (head + 1) * HD)
            queries_ref[:, at] = queries
            keyvals_ref[:, at] = keyvals
            probs_ref[head] = softmax_of(queries, keyvals)

    results = [((tokens, depth // 2), BF16)] * 2 + [((heads, tokens, tokens), F32)]
    return run(kernel, (x, total, gain), results, after)


def backward(x, gain, queries, keyvals, probs, grads, after):
    tokens, depth = x.shape

    def kernel(x_ref, gain_ref, queries_ref, keyvals_ref, probs_ref, *refs):
        grad_refs, (scaled_ref, moment_ref) = refs[:-2], refs[-2:]
        sums = jnp.zeros((tokens, HD), F32)
        half = tokens // 2
        for head in range(depth // (2 * HD)):
            at = slice(head * HD, (head + 1) * HD)
            queries, keyvals, probs = queries_ref[:, at], keyvals_ref[:, at], probs_ref[head]
            grad = grad_refs[0][:, at]
            if len(grad_refs) > 1 and grad_refs[1].shape[0] == half:
                arrived = jnp.concatenate([ref[:, at] for ref in grad_refs[1:]], axis=0)
                grad = grad + arrived.astype(F32)
            else:
                for ref in grad_refs[1:]:
                    grad = grad + ref[:, at].astype(F32)
            grad = grad.astype(BF16)
            dprob = dot(grad, keyvals, ((1,), (1,)))
            dvalue = dot(probs.astype(BF16), grad, ((0,), (0,)))
            inner = jnp.sum(dprob * probs, axis=-1, keepdims=True)
            dscore = (probs * (dprob - inner) * SHRINK).astype(BF16)
            dquery = dot(dscore, keyvals, ((1,), (0,)))
            dkeyval = dvalue + dot(dscore, queries, ((0,), (0,)))
            for start, value in ((0, dquery), (HD, dkeyval)):
                to = slice(head * 2 * HD + start, head * 2 * HD + start + HD)
                scaled = value * gain_ref[:, to]
                scaled_ref[:, to] = scaled
                sums = sums + scaled * x_ref[:, to].astype(F32)
        moment_ref[...] = as_row(sums)

    results = [((tokens, depth), F32), ((1, tokens), F32)]
    return run(kernel, (x, gain, queries, keyvals, probs, *grads), results, after)


def finish(rows, x, scaled, total, moments, width, parked, after):
    tokens, depth = rows.shape

    def body(parked_ref, rows_ref, x_ref, scaled_ref, total_ref, *refs):
        out_ref, moved_ref, held_ref, sems = refs[-4:]
        copies = [pltpu.make_async_copy(parked_ref, moved_ref, sems.at[0])]
        copies[0].start()
        moment = refs[0][...]
        for ref in refs[1 : len(moments)]:
            moment = moment + ref[...]
        inverse = lax.rsqrt(total_ref[...] / width + EPSILON)
        pull = as_column(inverse**3 * moment / width)
        inverse = as_column(inverse)
        for turn, start in enumerate(range(0, depth, 2 * HD)):
            for part in (start, start + HD):
                at = slice(part, part + HD)
                grad = rows_ref[:, at].astype(F32) + inverse * scaled_ref[:, at]
                held_ref[:, at] = (grad - x_ref[:, at].astype(F32) * pull).astype(BF16)
            at = slice(start, start + 2 * HD)
            copy = pltpu.make_async_copy(held_ref.at[:, at], out_ref.at[:, at], sems.at[1 + turn])
            copy.start()
            copies.append(copy)
        for copy in copies:
            copy.wait()

    return pl.pallas_call(
        body,
        in_specs=[VMEM] * (5 + len(moments) + len(after)),
        out_specs=[HBM, HBM],
        out_shape=[jax.ShapeDtypeStruct((tokens, depth), BF16)] * 2,
        scratch_shapes=[
            pltpu.VMEM((tokens, depth), BF16),
            pltpu.SemaphoreType.DMA((1 + depth // (2 * HD),)),
        ],
        compiler_params=pltpu.CompilerParams(vmem_limit_bytes=ROOM),
        name="finish",
    )(parked, rows, x, scaled, total, *moments, *after)


def piece(size, most):
    fits = [p for p in range(128, min(size, most) + 1, 128) if size % p == 0]
    return fits[-1] if fits else size


def project(plan, weight, contexts, offsets, chunk, base, after):
    tokens, width = contexts[0].shape[0], weight.shape[1]

    def kernel(weight_ref, *refs):
        total = None
        for context, offset in zip(refs, offsets):
            at = first_row(plan, offset, chunk)
            term = dot(context[...], weight_ref[pl.ds(at, chunk), :], ((1,), (0,)))
            total = term if total is None else total + term
        if base is not None:
            total = refs[len(offsets)][...] + total
        refs[-1][...] = total

    operands = (weight, *contexts) + (() if base is None else (base,))
    return run(kernel, operands, [((tokens, width), F32)], after)[0]


def project_last(plan, weight, contexts, offsets, chunk, base, fresh, after):
    tokens, width = fresh.shape
    block = piece(width, 512)
    halves = contexts[0].shape[0] != tokens

    def body(weight_ref, base_ref, fresh_ref, *refs):
        parts, (out_ref, held_ref, sems) = refs[: len(contexts)], refs[-3:]
        copies = []
        for turn, start in enumerate(range(0, width, block)):
            cols = slice(start, start + block)
            if halves:
                at = first_row(plan, offsets[0], chunk)
                weights = weight_ref[pl.ds(at, chunk), cols]
                total = jnp.concatenate([dot(p[...], weights, ((1,), (0,))) for p in parts], axis=0)
            else:
                total = jnp.zeros((tokens, block), F32)
                for context, offset in zip(parts, offsets):
                    at = first_row(plan, offset, chunk)
                    total += dot(context[...], weight_ref[pl.ds(at, chunk), cols], ((1,), (0,)))
            total = fresh_ref[:, cols].astype(F32) + (base_ref[:, cols] + total)
            held_ref[:, cols] = total.astype(BF16)
            copy = pltpu.make_async_copy(held_ref.at[:, cols], out_ref.at[:, cols], sems.at[turn])
            copy.start()
            copies.append(copy)
        for copy in copies:
            copy.wait()

    return pl.pallas_call(
        body,
        in_specs=[VMEM] * (3 + len(contexts) + len(after)),
        out_specs=HBM,
        out_shape=jax.ShapeDtypeStruct((tokens, width), BF16),
        scratch_shapes=[
            pltpu.VMEM((tokens, width), BF16),
            pltpu.SemaphoreType.DMA((width // block,)),
        ],
        compiler_params=pltpu.CompilerParams(vmem_limit_bytes=ROOM),
        name="last",
    )(weight, base, fresh, *contexts, *after)


def mirrored(value):
    sections = lax.axis_size("section")
    return lax.ppermute(value, "section", [(i, sections - 1 - i) for i in range(sections)])


def stages(size, factors):
    found = []
    while size > 1:
        factor = next((f for f in factors if size % f == 0), size)
        size //= factor
        found.append((size, factor))
    return found


def exchanged(value, stage, size):
    stride, factor = stage
    terms = [value]
    for turn in range(1, factor):
        pairs = []
        for i in range(size):
            digit = (i // stride) % factor
            pairs.append((i, i + ((digit + turn) % factor - digit) * stride))
        terms.append(lax.ppermute(value, "fsdp", pairs))
    return terms


def local(order, section_input, stash_held, upstream, norm_gain, out_weight):
    fresh, held, rows = section_input[0], stash_held[0], upstream[0]
    gain, weight = norm_gain, out_weight[0]
    count = len(order)
    tokens = fresh.shape[0]
    width = fresh.shape[1] * count
    chunk = weight.shape[0] // count
    half = tokens // 2
    far = (count - 1) // 2
    opposite = count % 2 == 0
    place = {device: at for at, device in enumerate(order)}
    plan = {
        offset: [order[(place[device] + offset) % count] for device in range(count)]
        for offset in range(-far, count // 2 + 1)
    }

    def turn(value, step):
        pairs = [(order[i], order[(i + step) % count]) for i in range(count)]
        return lax.ppermute(value, "fsdp", pairs)

    sums = squares(section_input, stash_held)
    last = sums
    fetched = mirrored(held)
    up = down = None
    if opposite:
        first = first_halves(plan, upstream, out_weight, count // 2, chunk, (last,))
        last = first[0]
        up = turn(first[0], 1)
        down = turn(first[1], -1 if count > 2 else 1)

    terms = [sums]
    for stage in stages(count, NARROW):
        terms = exchanged(functools.reduce(jnp.add, terms), stage, count)
    total_b = mirrored(functools.reduce(jnp.add, [t[1:2] for t in terms]))

    context = None
    for distance in range(far, 0, -1):
        pair = partial_sums(plan, rows, weight, (distance, -distance), chunk, (last,))
        last = pair[0]
        if distance == 1:
            own = partial_sums(plan, rows, weight, (0,), chunk, (last,))[0]
            last = own
        to_up, to_down = add_arrived(*pair, up, down, (last,))
        last = to_up
        up = turn(to_up, 1)
        down = turn(to_down, -1)
        if distance == far:
            context = forward(fresh, terms, gain, width, (last,))
            last = context
    if far == 0:
        own = partial_sums(plan, rows, weight, (0,), chunk, (last,))[0]
        context = forward(fresh, terms, gain, width, (own,))
    grads = [own] if up is None else [own, up, down]

    queries, keyvals, probs = prepare(fetched, total_b, gain, width, (last,))
    last = queries
    projected = None
    ahead = behind = context
    arrived, offsets = [context], [0]
    scaled = None
    for distance in range(1, far + 1):
        ahead, behind = turn(ahead, 1), turn(behind, -1)
        arrived += [ahead, behind]
        offsets += [-distance, distance]
        if distance < far or opposite:
            projected = project(plan, weight, arrived, offsets, chunk, projected, (last,))
            last = projected
            arrived, offsets = [], []
        if scaled is None:
            scaled, moment = backward(
                fetched, gain, queries, keyvals, probs, grads, (last,)
            )
            last = scaled
    if scaled is None:
        scaled, moment = backward(fetched, gain, queries, keyvals, probs, grads, (last,))
    moments = [moment]
    for stage in stages(count, WIDE):
        moments = exchanged(functools.reduce(jnp.add, moments), stage, count)
    moved = mirrored(fresh)
    grad_in, parked = finish(rows, fetched, scaled, total_b, moments, width, moved, ())
    if projected is None:
        if arrived:
            projected = project(plan, weight, arrived, offsets, chunk, None, ())
            arrived, offsets = [], []
    if opposite:
        ahead = turn(ahead[:half], 1)
        behind = turn(behind[half:], -1 if count > 2 else 1)
        arrived, offsets = [ahead, behind], [count // 2]
    output = project_last(plan, weight, arrived, offsets, chunk, projected, fresh, ())
    return (output[None], parked[None], grad_in[None])


def solution(mesh):
    order = ring_order(mesh)
    placed = P("section", None, "fsdp")

    def body(*arrays):
        return local(order, *arrays)

    return jax.shard_map(
        body,
        mesh=mesh,
        in_specs=(placed, placed, placed, P("section", "fsdp"), placed),
        out_specs=(placed, placed, placed),
        check_vma=False,
    )
```
